32 devices in a mesh: items: 8 (over z, y), band: 4 (over x, core).
Axes of the slice: x: 2, y: 2, z: 4, core: 2. Of those that a mesh axis runs over, the one named last changes fastest.
Arguments:
- activations: bfloat16 [24, 576, 768], P('items', 'band'), may hold values from -6 to 6
- heights: int32 [24], P('items'), may hold values from 12 to 24
- w_query: bfloat16 [768, 768], replicated, may hold values from -0.21875 to 0.21875
- w_key: bfloat16 [768, 768], replicated, may hold values from -0.21875 to 0.21875
- w_value: bfloat16 [768, 768], replicated, may hold values from -0.21875 to 0.21875
- w_out: bfloat16 [768, 768], replicated, may hold values from -0.875 to 0.875
- w_gate: bfloat16 [768, 2048], replicated, may hold values from -0.21875 to 0.21875
- w_up: bfloat16 [768, 2048], replicated, may hold values from -0.21875 to 0.21875
- w_down: bfloat16 [2048, 768], replicated, may hold values from -0.125 to 0.125
- first_gain: float32 [768], replicated, may hold values from 0.1 to 1.9
- second_gain: float32 [768], replicated, may hold values from 0.1 to 1.9
- cotangent: bfloat16 [24, 576, 768], P('items', 'band'), may hold values from -6 to 6
Outputs:
- output: bfloat16 [24, 576, 768], P('items', 'band')
- input_grad: bfloat16 [24, 576, 768], P('items', 'band')
- grad_query: float32 [768, 768], P(None, 'items')
- grad_key: float32 [768, 768], P(None, 'items')
- grad_value: float32 [768, 768], P(None, 'items')
- grad_out: float32 [768, 768], P(None, 'items')
- grad_gate: float32 [768, 2048], P(None, 'items')
- grad_up: float32 [768, 2048], P(None, 'items')
- grad_down: float32 [2048, 768], P(None, 'items')
- grad_first: float32 [768], P('items')
- grad_second: float32 [768], P('items')
The draws below stay inside these ranges and needn't reach their ends.
All inputs are finite; a program needn't handle non-finite values.
Results may differ from the reference program's by a relative error of at most 0.014.
Values may be sent and summed in bfloat16 or wider, within the bound.
No kernel may reach another device: no remote copies, remote signals or barrier semaphores. Data moves between devices by JAX's collectives and lax.ppermute only.
A program may use at most 192 MiB of HBM per device.

```python
import math
import jax
import jax.numpy as jnp
from jax import lax

D = 768
HEADS = 12
HEAD_DIM = 64
FF = 2048
ROWS = 24
COLS = 24
SLOTS = 576
ITEMS = 24


def with_ends(values, stream_key, low, top_value):
    extent = values.shape
    place = [jax.random.randint(jax.random.fold_in(stream_key, axis), (), 0, extent[axis]) for axis in range(len(extent))]
    values = values.at[tuple(place)].set(low)
    longest = extent.index(max(extent))
    place[longest] = (place[longest] + 1) % extent[longest]
    return values.at[tuple(place)].set(top_value)


def with_spikes(drawn, key, source, target, parts, factor):
    def block_of(dim):
        return (jnp.arange(drawn.shape[dim]) // (drawn.shape[dim] // parts)).reshape((-1,) + (1,) * (drawn.ndim - 1 - dim))

    one_side = jax.random.permutation(key, parts)[block_of(target)]
    far = (block_of(target) + parts // 2) % parts
    return jnp.where((block_of(source) == one_side) | (block_of(source) == far), factor * drawn, drawn)


def block_scale(key, dims, shards, least, top_value):
    def one(position, blocks):
        steps = jax.random.uniform(jax.random.fold_in(jax.random.fold_in(key, 6), position), (blocks,), jnp.float32, least / len(shards), top_value / len(shards))
        return jnp.repeat(jnp.exp(steps), dims[position] // blocks).reshape((-1,) + (1,) * (len(dims) - position - 1))

    level = one(*shards[0])
    for cut in shards[1:]:
        level = level * one(*cut)
    return level


def scatter_about(own_key, shape, scale, most, cuts=(), kind=jnp.bfloat16):
    gain = block_scale(own_key, shape, cuts, -0.22, 0.18) if cuts else 1.0
    entries = jax.random.normal(own_key, shape, jnp.float32) * scale * gain
    return jnp.minimum(jnp.maximum(entries, -most), most).astype(kind)


def heavy_noise(key, dims, deviation, bound, cuts, heavy, kind=jnp.bfloat16):
    values = deviation * jax.random.normal(key, dims, jnp.float32)
    if cuts:
        values = values * block_scale(key, dims, cuts, -0.22, 0.18)
    return jnp.clip(with_spikes(values, jax.random.fold_in(key, 3), *heavy), -bound, bound).astype(kind)


def setup_inputs(seed: int = 0) -> dict:
    seeds = jax.random.split(jax.random.key(seed), 13)
    return {
        "activations": scatter_about(seeds[0], (ITEMS, SLOTS, D), 1.0, 6.0, ((0, 8), (1, 4))),
        "heights": with_ends(jax.random.randint(seeds[1], (ITEMS,), ROWS // 2, ROWS + 1), jax.random.fold_in(seeds[1], 1), ROWS // 2, ROWS).astype(jnp.int32),
        "w_query": scatter_about(seeds[2], (D, D), D ** -0.5, 0.21875),
        "w_key": scatter_about(seeds[3], (D, D), D ** -0.5, 0.21875),
        "w_value": scatter_about(seeds[4], (D, D), D ** -0.5, 0.21875),
        "w_out": scatter_about(seeds[5], (D, D), (D // 16) ** -0.5, 0.875),
        "w_gate": scatter_about(seeds[6], (D, FF), D ** -0.5, 0.21875),
        "w_up": scatter_about(seeds[7], (D, FF), D ** -0.5, 0.21875),
        "w_down": scatter_about(seeds[8], (FF, D), FF ** -0.5, 0.125),
        "first_gain": jnp.clip(1.0 + 0.18 * jax.random.normal(seeds[9], (D,), jnp.float32), 0.1, 1.9),
        "second_gain": jnp.clip(1.0 + 0.18 * jax.random.normal(seeds[10], (D,), jnp.float32), 0.1, 1.9),
        "cotangent": heavy_noise(seeds[11], (ITEMS, SLOTS, D), 1.0, 6.0, ((0, 8), (1, 4)), (0, 2, 8, 2.0)),
    }


EPSILON = 1e-05
PRECISE = lax.Precision.HIGHEST

@jax.custom_vjp
def low(v):
    return lax.optimization_barrier(v.astype(jnp.bfloat16)).astype(jnp.float32)

@jax.custom_vjp
def low_back(v):
    return v

def low_keep(v):
    return (low(v), None)

def low_pass(kept, grad):
    return (grad,)

def back_keep(v):
    return (v, None)

def back_low(kept, grad):
    return (low(grad),)
low.defvjp(low_keep, low_pass)
low_back.defvjp(back_keep, back_low)

def product(left_side, right_side):
    return jnp.einsum('bsd,de->bse', left_side, right_side, precision=PRECISE)

def rotate(row_data, cosine_table, sine_table):
    half_dim = row_data.shape[-1] // 2
    first_half = row_data[..., :half_dim]
    second_half = row_data[..., half_dim:]
    return jnp.concatenate([first_half * cosine_table - second_half * sine_table, second_half * cosine_table + first_half * sine_table], axis=-1)

def tables(positions):
    half_dim = HEAD_DIM // 2
    frequency = jnp.exp(-math.log(10000.0) * (2.0 * jnp.arange(half_dim, dtype=jnp.float32) / HEAD_DIM))
    angles = positions[:, None] * frequency[None, :]
    return (jnp.cos(angles)[:, None, :], jnp.sin(angles)[:, None, :])

def block_forward(input_rows, w_query, w_key, w_value, w_out, w_gate, w_up, w_down, first_gain, second_gain, valid_rows, cosine_table, sine_table, allowed):
    groups, slot_count, width = input_rows.shape
    split_shape = (groups, slot_count, HEADS, HEAD_DIM)
    first_scale = lax.rsqrt(lax.optimization_barrier(jnp.mean(input_rows * input_rows, axis=-1, keepdims=True)) + EPSILON)
    normed = low(input_rows * first_scale * first_gain)
    query_raw = low_back(product(normed, w_query)).reshape(split_shape)
    key_raw = low_back(product(normed, w_key)).reshape(split_shape)
    value_rows = low(low_back(product(normed, w_value))).reshape(split_shape)
    query_rot = low(rotate(query_raw, cosine_table, sine_table) * HEAD_DIM ** (-0.5))
    key_rot = low(rotate(key_raw, cosine_table, sine_table))
    scores = low_back(jnp.einsum('bshd,bthd->bsht', query_rot, key_rot, precision=PRECISE))
    scores = jnp.where(allowed, scores, -1e+30)
    row_max = lax.optimization_barrier(jnp.max(scores, axis=-1, keepdims=True))
    exponent = jnp.exp(scores - row_max)
    prob_rows = low(exponent / lax.optimization_barrier(jnp.sum(exponent, axis=-1, keepdims=True)))
    attended = jnp.einsum('bsht,bthd->bshd', prob_rows, value_rows, precision=PRECISE)
    attended = low_back(low(attended.reshape(groups, slot_count, width)))
    residual = input_rows + low_back(product(attended, w_out))
    second_scale = lax.rsqrt(lax.optimization_barrier(jnp.mean(residual * residual, axis=-1, keepdims=True)) + EPSILON)
    normed_two = low(residual * second_scale * second_gain)
    gate_proj = low_back(product(normed_two, w_gate))
    up_proj = low_back(product(normed_two, w_up))
    hidden = low(jax.nn.silu(gate_proj) * up_proj)
    return valid_rows * (residual + low_back(product(hidden, w_down)))

def reference(activations, heights, w_query, w_key, w_value, w_out, w_gate, w_up, w_down, first_gain, second_gain, cotangent):
    weights = (w_query.astype(jnp.float32), w_key.astype(jnp.float32), w_value.astype(jnp.float32), w_out.astype(jnp.float32), w_gate.astype(jnp.float32), w_up.astype(jnp.float32), w_down.astype(jnp.float32), first_gain.astype(jnp.float32), second_gain.astype(jnp.float32))
    slot_index = jnp.arange(SLOTS, dtype=jnp.int32)
    cosine_table, sine_table = tables(slot_index.astype(jnp.float32))
    causal = slot_index[None, :] <= slot_index[:, None]
    group_size = math.gcd(ITEMS, 4)
    count = ITEMS // group_size
    grouped_inputs = activations.reshape(count, group_size, SLOTS, D)
    grouped_heights = heights.reshape(count, group_size)
    grouped_cot = cotangent.reshape(count, group_size, SLOTS, D)

    def one_group(totals, pieces):
        input_block, height_block, cot_block = pieces
        valid_bool = slot_index[None, :] // COLS < height_block[:, None]
        valid_rows = valid_bool.astype(jnp.float32)[:, :, None]
        allowed = causal[None, :, None, :] & valid_bool[:, None, None, :]

        def forward(input_rows, wq_full, wk_full, wv_full, wo_full, wg_full, wu_full, wd_full, gain_one, gain_two):
            return block_forward(input_rows, wq_full, wk_full, wv_full, wo_full, wg_full, wu_full, wd_full, gain_one, gain_two, valid_rows, cosine_table, sine_table, allowed)
        result, pullback = jax.vjp(forward, input_block.astype(jnp.float32), *weights)
        gradients = pullback(cot_block.astype(jnp.float32))
        new_totals = tuple((total + piece for total, piece in zip(totals, gradients[1:])))
        return (new_totals, (result.astype(jnp.bfloat16), gradients[0].astype(jnp.bfloat16)))
    start = tuple((jnp.zeros(weight.shape, jnp.float32) for weight in weights))
    totals, (outputs, input_grads) = lax.scan(one_group, start, (grouped_inputs, grouped_heights, grouped_cot))
    return (outputs.reshape(ITEMS, SLOTS, D), input_grads.reshape(ITEMS, SLOTS, D), totals[0], totals[1], totals[2], totals[3], totals[4], totals[5], totals[6], totals[7], totals[8])
```

```python
import functools
import math

import jax
import jax.numpy as jnp
from jax import lax
from jax.experimental import pallas as pl
from jax.experimental.pallas import tpu as pltpu
from jax.sharding import PartitionSpec as P

HEAD_DIM = 64
COLS = 24
EPSILON = 1e-05
LANES = 128
GROUP = 256
NEG = -1e30
AXES = ("items", "band")
BF16 = jnp.bfloat16
F32 = jnp.float32


def dot_nn(a, b):
    return lax.dot_general(a, b, (((1,), (0,)), ((), ())), preferred_element_type=F32)


def dot_nt(a, b):
    return lax.dot_general(a, b, (((1,), (1,)), ((), ())), preferred_element_type=F32)


def dot_tn(a, b):
    return lax.dot_general(a, b, (((0,), (0,)), ((), ())), preferred_element_type=F32)


def rope_tables(slots):
    half = HEAD_DIM // 2
    frequency = jnp.exp(
        -math.log(10000.0) * (2.0 * jnp.arange(half, dtype=F32) / HEAD_DIM)
    )
    angles = jnp.arange(slots, dtype=F32)[:, None] * frequency[None, :]
    cosine, sine = jnp.cos(angles), jnp.sin(angles)
    return (
        jnp.concatenate([cosine] * 4, axis=1),
        jnp.concatenate([-sine, sine, -sine, sine], axis=1),
    )


def turn(z, cosine, sine):
    lane = lax.broadcasted_iota(jnp.int32, z.shape, 1)
    low = (lane % HEAD_DIM) < HEAD_DIM // 2
    other = jnp.where(
        low, pltpu.roll(z, LANES - HEAD_DIM // 2, 1), pltpu.roll(z, HEAD_DIM // 2, 1)
    )
    return z * cosine + other * sine


def mask_bias(slots, tokens):
    row = lax.broadcasted_iota(jnp.int32, (slots, slots), 0)
    column = lax.broadcasted_iota(jnp.int32, (slots, slots), 1)
    return jnp.where((column <= row) & (column < tokens), 0.0, NEG).astype(F32)


def row_blocks(slots):
    step = slots // 3
    blocks = []
    for r in range(3):
        keys = min(slots, -(-(step * (r + 1)) // LANES) * LANES)
        blocks.append((r * step, step, keys))
    return blocks


BAND, CORE, SIDE, TOKENS, COUNTED, ITEM = range(6)


def join(place_ref, pieces, out_ref):
    band = place_ref[BAND]
    size = pieces[0].shape[0]
    for n, piece in enumerate(pieces):
        start = pl.multiple_of((band ^ n) * size, 16)
        out_ref[pl.ds(start, size), :] = piece[...]


def forward_kernel(
    place_ref, p0_ref, p1_ref, p2_ref, p3_ref, gain_ref, cos_ref, sin_ref, wq_ref, wk_ref, wv_ref,
    x_ref, q_ref, k_ref, v_ref, lse_ref, att_ref, normed_scr, bias_scr,
):
    slots, width = x_ref.shape
    join(place_ref, (p0_ref, p1_ref, p2_ref, p3_ref), x_ref)
    x = x_ref[...].astype(F32)
    r1 = lax.rsqrt(jnp.mean(x * x, axis=-1, keepdims=True) + EPSILON)
    normed_scr[...] = (x * r1 * gain_ref[...]).astype(BF16)
    bias_scr[...] = mask_bias(slots, place_ref[TOKENS])

    def group(g, carry):
        columns = pl.ds(pl.multiple_of(g * GROUP, GROUP), GROUP)
        normed = normed_scr[...]
        cosine, sine = cos_ref[...], sin_ref[...]
        q_all = dot_nn(normed, wq_ref[:, columns])
        k_all = dot_nn(normed, wk_ref[:, columns])
        v_all = dot_nn(normed, wv_ref[:, columns]).astype(BF16)
        v_ref[:, columns] = v_all
        for p in range(GROUP // LANES):
            cut = slice(p * LANES, (p + 1) * LANES)
            place = pl.ds(pl.multiple_of(g * GROUP + p * LANES, LANES), LANES)
            q2 = (turn(q_all[:, cut], cosine, sine) * HEAD_DIM ** (-0.5)).astype(BF16)
            k2 = turn(k_all[:, cut], cosine, sine).astype(BF16)
            v2 = v_all[:, cut]
            q_ref[:, place] = q2
            k_ref[:, place] = k2
            low_v = lax.broadcasted_iota(jnp.int32, v2.shape, 1) < HEAD_DIM
            one = jnp.ones_like(v2)
            v_ext = (jnp.where(low_v, v2, one), jnp.where(low_v, one, v2))
            for start, size, keys in row_blocks(slots):
                rows = slice(start, start + size)
                low = low_v[rows]
                zero = jnp.zeros((size, LANES), BF16)
                outs, logs = [], []
                for head in range(2):
                    qh = jnp.where(low, q2[rows], zero) if head == 0 else jnp.where(low, zero, q2[rows])
                    s = dot_nt(qh, k2[:keys]) + bias_scr[rows, :keys]
                    m = jnp.max(s, axis=-1, keepdims=True)
                    e = jnp.exp(s - m).astype(BF16)
                    o = dot_nn(e, v_ext[head][:keys])
                    total = o[:, HEAD_DIM : HEAD_DIM + 1] if head == 0 else o[:, 0:1]
                    outs.append(o / total)
                    logs.append(jnp.broadcast_to(m + jnp.log(total), o.shape))
                att_ref[rows, place] = jnp.where(low, outs[0], outs[1]).astype(BF16)
                lse_ref[rows, place] = jnp.where(low, logs[0], logs[1])
        return carry

    lax.fori_loop(0, width // GROUP, group, 0)

def halves(place_ref, value_ref, units, keep_ref, send_ref):
    rows = value_ref.shape[0] // units // 2
    for n in range(units):
        for ref, core in ((keep_ref, place_ref[CORE]), (send_ref, 1 - place_ref[CORE])):
            start = pl.multiple_of((2 * n + core) * rows, 16)
            ref[n * rows : (n + 1) * rows, :] = value_ref[pl.ds(start, rows), :]


def middle_kernel(
    place_ref, x_ref, att_ref, wo_ref, gain_ref, res_ref, n2_ref, keep_ref, send_ref, scr
):
    res = x_ref[...].astype(F32) + dot_nn(att_ref[...], wo_ref[...])
    res_ref[...] = res
    r2 = lax.rsqrt(jnp.mean(res * res, axis=-1, keepdims=True) + EPSILON)
    n2 = res * r2 * gain_ref[...]
    n2_ref[...] = n2.astype(BF16)
    scr[...] = n2.T.astype(BF16)
    halves(place_ref, scr, 2, keep_ref, send_ref)


def middle(place, x, att, wo, gain):
    slots, width = x.shape
    rows = (slots, width)
    half = (width // 2, slots)
    return kernel_call(
        middle_kernel, "middle", (place, x, att, wo, gain),
        [(rows, F32), (rows, BF16), (half, BF16), (half, BF16)], [((width, slots), BF16)],
        flops=2 * slots * width * width, scalars=1, limit=6,
    )


VMEM = pl.BlockSpec(memory_space=pltpu.VMEM)
SMEM = pl.BlockSpec(memory_space=pltpu.SMEM)
ANY = pl.BlockSpec(memory_space=pl.ANY)
HBM = pl.BlockSpec(memory_space=pltpu.HBM)


def kernel_call(
    body, name, operands, outs, scratch=(), limit=2, flops=0, scalars=0, source=VMEM, target=VMEM,
    semaphores=0,
):
    shapes = [jax.ShapeDtypeStruct(shape, kind) for shape, kind in outs]
    single = len(shapes) == 1
    scratch = [pltpu.VMEM(shape, kind) for shape, kind in scratch]
    if semaphores:
        scratch.append(pltpu.SemaphoreType.DMA((semaphores,)))
    return pl.pallas_call(
        body,
        in_specs=[SMEM] * scalars + [source] * (len(operands) - scalars),
        out_specs=target if single else [target] * len(shapes),
        out_shape=shapes[0] if single else shapes,
        scratch_shapes=scratch,
        compiler_params=pltpu.CompilerParams(vmem_limit_bytes=limit << 20),
        cost_estimate=pl.CostEstimate(flops=1, bytes_accessed=1, transcendentals=0),
        name=name,
    )(*operands)


def forward(place, pieces, gain, cosine, sine, wq, wk, wv):
    width = wq.shape[0]
    slots = 4 * pieces[0].shape[0]
    rows = (slots, width)
    return kernel_call(
        forward_kernel, "attention_forward",
        (place, *pieces, gain, cosine, sine, wq, wk, wv),
        [(rows, BF16)] * 4 + [(rows, F32), (rows, BF16), (rows, BF16), ((slots, slots), F32)],
        flops=14 * slots * width * width, scalars=1, limit=8,
    )


def branch_kernel(
    units, place_ref, p0_ref, p1_ref, p2_ref, p3_ref, branch_ref, keep_ref, send_ref, scr
):
    join(place_ref, (p0_ref, p1_ref, p2_ref, p3_ref), branch_ref)
    value = branch_ref[...].astype(F32)
    slot = lax.broadcasted_iota(jnp.int32, value.shape, 0)
    value = jnp.where(slot < place_ref[COUNTED], value, 0.0)
    branch_ref[...] = value.astype(BF16)
    scr[...] = value.T.astype(BF16)
    halves(place_ref, scr, units, keep_ref, send_ref)


def branch_rows(place, pieces, shards):
    band_slots, width = pieces[0].shape
    slots = 4 * band_slots
    half = (width // 2, slots)
    units = shards if (width // shards) % 32 == 0 else 1
    return kernel_call(
        functools.partial(branch_kernel, units), "branch_rows", (place, *pieces),
        [((slots, width), BF16), (half, BF16), (half, BF16)], [((width, slots), BF16)],
        scalars=1, flops=slots * width, limit=4,
    )


def hidden_kernel(n2_ref, branch_ref, wg_ref, wu_ref, wd_ref, hid_ref, gg_ref, gu_ref):
    def block(j, carry):
        columns = pl.ds(pl.multiple_of(j * GROUP, GROUP), GROUP)
        n2 = n2_ref[...]
        gate = dot_nn(n2, wg_ref[:, columns])
        up = dot_nn(n2, wu_ref[:, columns])
        grad_hidden = dot_nt(branch_ref[...], wd_ref[columns, :])
        sig = jax.nn.sigmoid(gate)
        silu = gate * sig
        hid_ref[:, columns] = (silu * up).astype(BF16)
        gg_ref[:, columns] = (grad_hidden * up * (sig * (1.0 + gate * (1.0 - sig)))).astype(BF16)
        gu_ref[:, columns] = (grad_hidden * silu).astype(BF16)
        return carry

    lax.fori_loop(0, wg_ref.shape[1] // GROUP, block, 0)


def hidden_rows(n2, branch, wg, wu, wd):
    slots, width = n2.shape
    ff = wg.shape[1]
    return kernel_call(
        hidden_kernel, "hidden_rows", (n2, branch, wg, wu, wd), [((slots, ff), BF16)] * 3,
        flops=6 * slots * width * ff, limit=3,
    )


def columns_kernel(lhs_ref, gate_ref, up_ref, out_ref):
    _, shards, rows, step = out_ref.shape
    rows //= 2
    for n, ref in enumerate((gate_ref, up_ref)):
        for i in range(0, shards, 2):
            out = dot_nn(lhs_ref[...], ref[:, i * step : (i + 2) * step]).astype(BF16)
            for j in range(2):
                part = out[:, j * step : (j + 1) * step].reshape(2, rows, step)
                out_ref[:, i + j, n * rows : (n + 1) * rows, :] = part


def grad_columns(lhs, gate, up, shards):
    half, slots = lhs.shape
    ff = gate.shape[1]
    step = ff // shards
    if step % LANES:
        parts = [
            dot_nn(lhs, value).astype(BF16).reshape(2, half // 2, shards, step) for value in (gate, up)
        ]
        return jnp.swapaxes(jnp.concatenate(parts, axis=1), 1, 2)
    return kernel_call(
        columns_kernel, "grad_columns", (lhs, gate, up), [((2, shards, half, step), BF16)],
        flops=4 * slots * half * ff, limit=4,
    )


def down_kernel(lhs_ref, rhs_ref, out_ref):
    _, shards, rows, half = out_ref.shape
    step = 2 * GROUP
    for start in range(0, 2 * half, step):
        out = dot_nn(lhs_ref[...], rhs_ref[:, start : start + step]).astype(BF16)
        side, at = divmod(start, half)
        out_ref[side, :, :, at : at + step] = out.reshape(shards, rows, step)


def grad_down(lhs, hidden, shards):
    half, slots = lhs.shape
    ff = hidden.shape[1]
    rows = half // shards
    if rows % 16:
        out = dot_nn(lhs, hidden).astype(BF16).reshape(shards, rows, 2, ff // 2)
        return jnp.transpose(out, (2, 0, 1, 3))
    return kernel_call(
        down_kernel, "grad_down", (lhs, hidden), [((2, shards, rows, ff // 2), BF16)],
        flops=2 * slots * half * ff, limit=4,
    )


def combine_kernel(stage, turn, extra, place_ref, held_ref, got_ref, *refs):
    if extra:
        refs[-1][...] = refs[0][...] + refs[1][...]
        out_refs = refs[2:-1]
    else:
        out_refs = refs
    count = out_refs[0].shape[0]
    if len(out_refs) == 1:
        stride, starts = 1, (0,)
    elif stage < 2:
        by_item = (place_ref[CORE] ^ turn ^ stage) & 1
        side = place_ref[SIDE]
        odd = place_ref[ITEM] & 1
        stride = 1 + by_item
        starts = [
            (1 - by_item) * (a * count) + by_item * b for a, b in ((side, odd), (1 - side, 1 - odd))
        ]
    else:
        mine = (place_ref[ITEM] >> (stage - 1)) & 1
        stride, starts = 2, (mine, 1 - mine)

    def one(j, carry):
        for start, out_ref in zip(starts, out_refs):
            at = j * stride + start
            out_ref[j] = (held_ref[at].astype(F32) + got_ref[at].astype(F32)).astype(BF16)
        return carry

    lax.fori_loop(0, count, one, 0)


def combine(place, held, got, stage, turn, split, extra=()):
    blocks, r, c = held.shape
    outs = [((blocks // 2, r, c), BF16)] * 2 if split else [((blocks, r, c), BF16)]
    outs += [(value.shape, value.dtype) for value in extra[:1]]
    out = kernel_call(
        functools.partial(combine_kernel, stage, turn, bool(extra)), "combine",
        (place, held, got, *extra), outs, flops=held.size, scalars=1, limit=3,
    )
    return out if isinstance(out, (list, tuple)) else [out]


def join_kernel(
    bit, place_ref, low_ref, held_ref, got_ref, gains_ref, more_ref, keep_ref, send_ref, sum_ref
):
    sum_ref[...] = gains_ref[...] + more_ref[...]
    value = (held_ref[...].astype(F32) + got_ref[...].astype(F32)).astype(BF16)
    mine = (place_ref[ITEM] >> bit) & 1
    for top in range(2):
        @pl.when(mine == top)
        def _():
            (keep_ref if top else send_ref)[...] = value
            (send_ref if top else keep_ref)[...] = low_ref[...]


def join_halves(place, low, held, got, gains, more, bit):
    outs = [(low.shape, BF16)] * 2 + [(gains.shape, F32)]
    return kernel_call(
        functools.partial(join_kernel, bit), "join_halves", (place, low, held, got, gains, more), outs,
        flops=low.size, scalars=1, limit=3,
    )


def pair_kernel(place_ref, a_ref, b_ref, *out_refs):
    for core in range(2):
        @pl.when(place_ref[CORE] == core)
        def _():
            out_refs[0][...] = (a_ref, b_ref)[core][...]
            out_refs[1][...] = (b_ref, a_ref)[core][...]


def pair(place, a, b):
    return kernel_call(
        pair_kernel, "pair", (place, a, b), [(a.shape, a.dtype)] * 2, flops=a.size, scalars=1, limit=1,
    )


def pick_kernel(place_ref, first_ref, second_ref, mine_ref, theirs_ref):
    for choice in range(3):
        left = place_ref[SIDE] == 0
        now = (left & (place_ref[CORE] == choice)) if choice < 2 else jnp.logical_not(left)
        @pl.when(now)
        def _():
            mine_ref[...] = (second_ref if choice == 1 else first_ref)[...]
            theirs_ref[...] = (second_ref if choice == 0 else first_ref)[...]


def pick(place, first, second):
    return kernel_call(
        pick_kernel, "pick", (place, first, second), [(first.shape, first.dtype)] * 2,
        flops=first.size, scalars=1, limit=1,
    )


def take_kernel(place_ref, rows_ref, own_ref, other_ref, far_ref, second_ref, sems):
    side, core = place_ref[SIDE], place_ref[CORE]
    wanted = (
        (jnp.where(side == 0, 2, 0), far_ref),
        (1, second_ref),
        (jnp.where(side == 0, 1 - core, 2), other_ref),
        (jnp.where(side == 0, core, 2), own_ref),
    )
    copies = [
        pltpu.make_async_copy(rows_ref.at[index], ref, sems.at[n])
        for n, (index, ref) in enumerate(wanted)
    ]
    for copy in copies:
        copy.start()
    for copy in copies:
        copy.wait()


def take(place, rows):
    _, size, width = rows.shape
    return kernel_call(
        take_kernel, "take", (place, rows), [((size, width), rows.dtype)] * 4,
        flops=size * width, scalars=1, limit=1, source=HBM, semaphores=4,
    )


def output_kernel(place_ref, hid_ref, wd_ref, res_ref, p0_ref, p1_ref, p2_ref, p3_ref, scr):
    out = res_ref[...] + dot_nn(hid_ref[...], wd_ref[...])
    slot = lax.broadcasted_iota(jnp.int32, out.shape, 0)
    scr[...] = jnp.where(slot < place_ref[TOKENS], out, 0.0).astype(BF16)
    part(place_ref, scr, (p0_ref, p1_ref, p2_ref, p3_ref))


def part(place_ref, value_ref, pieces):
    band = place_ref[BAND]
    size = pieces[0].shape[0]
    for n, piece in enumerate(pieces):
        start = pl.multiple_of((band ^ n) * size, 16)
        piece[...] = value_ref[pl.ds(start, size), :]


def output_rows(place, hidden, wd, res):
    slots, width = res.shape
    return kernel_call(
        output_kernel, "output_rows", (place, hidden, wd, res),
        [((slots // 4, width), BF16)] * 4, [((slots, width), BF16)],
        flops=2 * slots * width * hidden.shape[1], scalars=1, limit=5,
    )


def copy_all(pairs, sems):
    copies = [
        pltpu.make_async_copy(source, target, sems.at[n]) for n, (source, target) in enumerate(pairs)
    ]
    for copy in copies:
        copy.start()
    for copy in copies:
        copy.wait()


def band_kernel(place_ref, own_ref, core_ref, first_ref, second_ref, out_ref, sems):
    for core in range(2):
        own, other = (own_ref, core_ref) if core == 0 else (core_ref, own_ref)

        @pl.when((place_ref[SIDE] == 0) & (place_ref[CORE] == core))
        def _():
            copy_all([(own, out_ref.at[0]), (other, out_ref.at[1]), (first_ref, out_ref.at[2])], sems)

        @pl.when((place_ref[SIDE] == 1) & (place_ref[CORE] == core))
        def _():
            copy_all(
                [(first_ref, out_ref.at[0]), (second_ref, out_ref.at[1]), (own, out_ref.at[2])], sems
            )


def band_rows(place, own, core, first, second):
    size, width = own.shape
    return kernel_call(
        band_kernel, "band_rows", (place, own, core, first, second),
        [((3, size, width), BF16)], flops=size * width, scalars=1, limit=1, target=ANY, semaphores=3,
    )


def rows_kernel(place_ref, p0_ref, p1_ref, p2_ref, p3_ref, gate_ref, up_ref, scr, sems):
    half = p0_ref.shape[0] // 2
    for n, piece in enumerate((p0_ref, p1_ref, p2_ref, p3_ref)):
        start = pl.multiple_of((place_ref[BAND] ^ n) * half, 8)
        scr[0, pl.ds(start, half), :] = piece[:half, :].astype(F32)
        scr[1, pl.ds(start, half), :] = piece[half:, :].astype(F32)
    copy_all([(scr.at[0], gate_ref), (scr.at[1], up_ref)], sems)


def stacked_rows(place, pieces):
    r, c = pieces[0].shape
    out = ((2 * r, c), F32)
    return kernel_call(
        rows_kernel, "weight_rows", (place, *pieces), [out, out], [((2, 2 * r, c), F32)],
        flops=4 * r * c, scalars=1, limit=4, target=ANY, semaphores=2,
    )


def down_out_kernel(place_ref, p0_ref, p1_ref, p2_ref, p3_ref, out_ref, scr, out_scr, sems):
    for n, piece in enumerate((p0_ref, p1_ref, p2_ref, p3_ref)):
        scr[place_ref[BAND] ^ n] = piece[...]
    r, c = p0_ref.shape
    for side in range(2):
        for core in range(2):
            out_scr[core * r : (core + 1) * r, side * c : (side + 1) * c] = (
                scr[2 * side + core].astype(F32)
            )
    copy_all([(out_scr, out_ref)], sems)


def down_out(place, pieces):
    r, c = pieces[0].shape
    shape = (2 * r, 2 * c)
    return kernel_call(
        down_out_kernel, "weight_down", (place, *pieces), [(shape, F32)],
        [((4, r, c), BF16), (shape, F32)], limit=4, scalars=1, target=ANY, semaphores=1,
    ).T


def attention_out_kernel(place_ref, p0_ref, p1_ref, p2_ref, p3_ref, *refs):
    outs, (scr, out_scr, sems) = refs[:4], refs[4:]
    for n, piece in enumerate((p0_ref, p1_ref, p2_ref, p3_ref)):
        scr[place_ref[BAND] ^ n] = piece[...]
    out_scr[...] = scr[...].astype(F32)
    copy_all([(out_scr.at[n], outs[n]) for n in range(4)], sems)


def attention_out(place, pieces):
    r, c = pieces[0].shape
    outs = kernel_call(
        attention_out_kernel, "weight_attention", (place, *pieces), [((r, c), F32)] * 4,
        [((4, r, c), BF16), ((4, r, c), F32)], limit=4, scalars=1, target=ANY, semaphores=4,
    )
    return [out.T for out in outs]


def gains_kernel(place_ref, a_ref, b_ref, first_ref, second_ref):
    total = a_ref[...] + b_ref[...]
    width = total.shape[1]
    share = first_ref.shape[1]
    for n in range(width // share):
        @pl.when(place_ref[ITEM] == n)
        def _():
            mine = total if n == 0 else pltpu.roll(total, width - n * share, 1)
            first_ref[...] = mine[0:1, :share]
            second_ref[...] = mine[1:2, :share]


def gains_out(place, a, b, shards):
    width = a.shape[1]
    out = ((1, width // shards), F32)
    return kernel_call(
        gains_kernel, "gains", (place, a, b), [out, out], flops=a.size, scalars=1, limit=1,
    )


def residual_kernel(
    gg_ref, gu_ref, wg_ref, wu_ref, res_ref, branch_ref, gain_ref, wo_ref, att_ref,
    gres_ref, gatt_ref, gwo_ref, gsec_ref,
):
    slots, width = res_ref.shape
    gn = dot_nt(gg_ref[...], wg_ref[...]) + dot_nt(gu_ref[...], wu_ref[...])
    res = res_ref[...]
    r2 = lax.rsqrt(jnp.mean(res * res, axis=-1, keepdims=True) + EPSILON)
    weighted = gain_ref[...] * gn
    inner = jnp.mean(res * weighted, axis=-1, keepdims=True)
    gsec_ref[...] = jnp.sum(gn * res * r2, axis=0, keepdims=True)
    gres = branch_ref[...].astype(F32) + r2 * weighted - res * (r2 * r2 * r2) * inner
    gres_ref[...] = gres
    low = gres.astype(BF16)
    gatt_ref[...] = dot_nt(low, wo_ref[...]).astype(BF16)
    gwo_ref[...] = dot_tn(low, att_ref[...]).astype(BF16)


def residual_grad(gg, gu, wg, wu, res, branch, gain, wo, att):
    slots, width = res.shape
    ff = gg.shape[1]
    rows = (slots, width)
    return kernel_call(
        residual_kernel, "residual_grad", (gg, gu, wg, wu, res, branch, gain, wo, att),
        [(rows, F32), (rows, BF16), ((width, width), BF16), ((1, width), F32)],
        flops=4 * slots * width * ff + 4 * slots * width * width, limit=5,
    )


def backward_kernel(
    pair_ref, bias_ref, cos_ref, sin_ref, q_ref, k_ref, v_ref, gatt_ref, att_ref, lse_ref,
    dq_ref, dk_ref, dv_ref,
):
    slots = q_ref.shape[0]
    cosine, sine = cos_ref[...], -sin_ref[...]
    place = pl.ds(pl.multiple_of(pair_ref[0] * LANES, LANES), LANES)
    k2, v2 = k_ref[:, place], v_ref[:, place]
    low_k = lax.broadcasted_iota(jnp.int32, k2.shape, 1) < HEAD_DIM
    none = jnp.zeros_like(k2)
    k_of = (jnp.where(low_k, k2, none), jnp.where(low_k, none, k2))
    dk = jnp.zeros((slots, LANES), F32)
    dv = jnp.zeros((slots, LANES), F32)
    for start, size, keys in row_blocks(slots):
        rows = slice(start, start + size)
        q2, do2 = q_ref[rows, place], gatt_ref[rows, place]
        prod = do2.astype(F32) * att_ref[rows, place].astype(F32)
        lse2 = lse_ref[rows, place]
        low = low_k[rows]
        zero = jnp.zeros_like(q2)
        dq = jnp.zeros((size, LANES), F32)
        dk_part = jnp.zeros((keys, LANES), F32)
        dv_part = jnp.zeros((keys, LANES), F32)
        for head in range(2):
            mine = low if head == 0 else jnp.logical_not(low)
            qh = jnp.where(mine, q2, zero)
            doh = jnp.where(mine, do2, zero)
            delta = jnp.sum(jnp.where(mine, prod, 0.0), axis=-1, keepdims=True)
            lse = lse2[:, head * HEAD_DIM : head * HEAD_DIM + 1]
            s = dot_nt(qh, k2[:keys]) + bias_ref[rows, :keys]
            prob = jnp.exp(s - lse)
            dp = dot_nt(doh, v2[:keys])
            ds = (prob * (dp - delta)).astype(BF16)
            prob = prob.astype(BF16)
            dv_part += dot_tn(prob, doh)
            dk_part += dot_tn(ds, qh)
            dq += dot_nn(ds, k_of[head][:keys])
        dq_ref[rows, :] = (
            turn(dq, cosine[rows], sine[rows]) * HEAD_DIM ** (-0.5)
        ).astype(BF16)
        if keys < slots:
            pad = jnp.zeros((slots - keys, LANES), F32)
            dk_part = jnp.concatenate([dk_part, pad], axis=0)
            dv_part = jnp.concatenate([dv_part, pad], axis=0)
        dk += dk_part
        dv += dv_part
    dk_ref[...] = turn(dk, cosine, sine).astype(BF16)
    dv_ref[...] = dv.astype(BF16)


def backward(p, bias, cosine, sine, q, k, v, gatt, att, lse):
    slots, width = q.shape
    return kernel_call(
        backward_kernel, "attention_backward",
        (jnp.full((1,), p, jnp.int32), bias, cosine, sine, q, k, v, gatt, att, lse),
        [((slots, LANES), BF16)] * 3, flops=28 * slots * slots * LANES, scalars=1, limit=6,
    )


def attention_weights_kernel(*refs):
    (place_ref, half_ref), refs = refs[:2], refs[2:]
    normed_ref, gwo_ref, keep_ref, send_ref = refs[-4:]
    grads = refs[:-4]
    shape = keep_ref.shape[1:]
    normed = normed_ref[...]

    def weight(n):
        value = jnp.concatenate([ref[...] for ref in grads[n::3]], axis=1)
        return dot_tn(value, normed).astype(BF16).reshape(shape)

    rows = shape[0] * shape[1]
    start = pl.multiple_of(half_ref[0] * rows, 16)
    for core in range(2):
        @pl.when(place_ref[CORE] == core)
        def _():
            even, odd = (keep_ref, send_ref) if core == 0 else (send_ref, keep_ref)
            even[0] = gwo_ref[pl.ds(start, rows), :].reshape(shape)
            odd[0] = weight(0)
            even[1] = weight(1)
            odd[1] = weight(2)


def attention_weights(place, half, grads, normed, gwo, shards):
    slots, width = normed.shape
    shape = (2, shards // 2, width // shards, width)
    if (width // shards) % 16:
        parts = [jnp.concatenate(grads[n::3], axis=1) for n in range(3)]
        weights = [dot_tn(value, normed).astype(BF16) for value in parts]
        rows = width // 2
        weights = jnp.stack([gwo[half * rows : (half + 1) * rows], *weights])
        parts = weights.reshape(2, 2, *shape[1:])
        return [
            lax.dynamic_index_in_dim(parts, core, 1, keepdims=False)
            for core in (place[CORE], 1 - place[CORE])
        ]
    return kernel_call(
        attention_weights_kernel, "attention_weights",
        (place, jnp.full((1,), half, jnp.int32), *grads, normed, gwo), [(shape, BF16)] * 2,
        flops=3 * slots * width * width, scalars=2, limit=6,
    )


def input_kernel(*refs):
    place_ref, refs = refs[0], refs[1:]
    count = len(refs) - 13
    grads, refs = refs[:count], refs[count:]
    wq_ref, wk_ref, wv_ref, x_ref, gain_ref, gres_ref, gsec_ref = refs[:7]
    pieces, (gains_ref, scr) = refs[7:11], refs[11:]
    gn = jnp.zeros(x_ref.shape, F32)
    for n, weight in enumerate((wq_ref, wk_ref, wv_ref)):
        value = jnp.concatenate([ref[...] for ref in grads[n::3]], axis=1)
        gn += dot_nt(value, weight[...])
    x = x_ref[...].astype(F32)
    r1 = lax.rsqrt(jnp.mean(x * x, axis=-1, keepdims=True) + EPSILON)
    weighted = gain_ref[...] * gn
    inner = jnp.mean(x * weighted, axis=-1, keepdims=True)
    first = jnp.sum(gn * x * r1, axis=0, keepdims=True)
    scr[...] = (gres_ref[...] + r1 * weighted - x * (r1 * r1 * r1) * inner).astype(BF16)
    part(place_ref, scr, pieces)
    gains_ref[...] = jnp.concatenate(
        [first, gsec_ref[...], jnp.zeros((6, first.shape[1]), F32)], axis=0
    )


def input_rows_grad(place, grads, wq, wk, wv, x, gain, gres, gsec):
    slots, width = x.shape
    return kernel_call(
        input_kernel, "input_grad", (place, *grads, wq, wk, wv, x, gain, gres, gsec),
        [((slots // 4, width), BF16)] * 4 + [((8, width), F32)],
        [((slots, width), BF16)],
        flops=6 * slots * width * width, scalars=1, limit=8,
    )


class Grid:
    def __init__(self, mesh):
        self.items = mesh.shape["items"]
        self.band = mesh.shape["band"]
        self.bits = self.items.bit_length() - 1

    def setup(self):
        self.i = lax.axis_index("items")
        self.b = lax.axis_index("band")
        self.core = self.b % 2
        self.x = self.b // 2
        self.y = self.i % 2
        self.last = ()

    def swap(self, value, partner, only=None):
        (value,) = self.after(value)
        pairs = []
        for i in range(self.items):
            for b in range(self.band):
                j, c = partner(i, b)
                if only is None or b // 2 == only:
                    pairs.append((i * self.band + b, j * self.band + c))
        return lax.ppermute(value, AXES, pairs)

    def swap_core(self, value):
        return self.swap(value, lambda i, b: (i, b ^ 1))

    def swap_x(self, value, only=None):
        return self.swap(value, lambda i, b: (i, b ^ 2), only)

    def swap_item(self, value, bit):
        return self.swap(value, lambda i, b: (i ^ (1 << bit), b))

    def swap_xy(self, value, turn):
        return self.swap(value, lambda i, b: (i ^ 1, b) if (b ^ turn) & 1 else (i, b ^ 2))

    def after(self, *values):
        if not self.last:
            return values
        tied = lax.optimization_barrier((values, self.last))
        return tied[0]

    def done(self, *values):
        self.last = values


class Reduction:
    def __init__(self, grid, sent, turn, bits):
        self.grid, self.turn, self.bits = grid, turn, bits
        self.sent = sent.reshape(-1, *sent.shape[2:])
        self.stage = 0
        self.over = False
        self.gains = self.more = None

    def keep(self, kept):
        self.held = kept.reshape(-1, *kept.shape[2:])
        self.grid.done(self.held)

    def exchange(self, value):
        grid = self.grid
        if self.stage == 0:
            return grid.swap_core(value)
        if self.stage <= 2:
            return grid.swap_xy(value, self.turn ^ self.stage ^ 1)
        return grid.swap_item(value, self.stage - 2)

    def start(self):
        self.got = self.exchange(self.sent)
        if self.gains is not None:
            self.more = self.exchange(self.gains)
        self.sent = None

    def finish(self):
        grid = self.grid
        extra = () if self.more is None else (self.gains, self.more)
        held, got, *extra = grid.after(self.held, self.got, *extra)
        self.over = self.stage == self.bits + 1
        out = combine(grid.place, held, got, self.stage, self.turn, not self.over, extra)
        if extra:
            *out, self.gains = out
        self.held = out[0]
        if not self.over:
            self.sent = out[1]
        self.stage += 1
        grid.done(self.held)

    def gather(self, block):
        grid = self.grid
        core = grid.swap_core(block)
        side = grid.swap_x(block)
        return block, core, side, grid.swap_core(side)


def exchange_band(grid, taken):
    own, other, far, second = taken
    first = grid.swap_x(far)
    second = grid.swap_x(second, only=1)
    core = grid.swap_core(other)
    return own, core, first, second


def body(
    grid, activations, heights, w_query, w_key, w_value, w_out, w_gate, w_up, w_down,
    first_gain, second_gain, cotangent,
):
    grid.setup()
    items = grid.items
    _, band_slots, width = activations.shape
    slots = band_slots * grid.band
    ff = w_gate.shape[1]
    share = width // items
    place = jnp.stack([grid.b, grid.core, grid.x, grid.x, grid.x, grid.i]).astype(jnp.int32)
    grid.place = place
    taken = take(place, activations)
    own, core, first, second = exchange_band(grid, taken)
    (cotangent,) = lax.optimization_barrier((cotangent, taken))[:1]
    cot_taken = take(place, cotangent)
    index = jnp.minimum(grid.b, 2)
    tokens = lax.dynamic_slice(heights, (index,), (1,))[0] * COLS
    counted = jnp.where(grid.b < 3, tokens, 0)
    place = jnp.stack([grid.b, grid.core, grid.x, tokens, counted, grid.i]).astype(jnp.int32)
    grid.place = place
    cosine, sine = rope_tables(slots)
    gain, gain_two = first_gain[None, :], second_gain[None, :]

    first, second, cosine, sine, gain, gain_two, cot_taken, _ = lax.optimization_barrier(
        (first, second, cosine, sine, gain, gain_two, cot_taken, place)
    )
    mine, theirs = pick(place, first, second)
    theirs = grid.swap_core(theirs)
    grid.done(mine)
    cot_pieces = exchange_band(grid, cot_taken)
    x, q, k, v, lse, att, normed, bias = forward(
        place, (own, core, mine, theirs), gain, cosine, sine, w_query, w_key, w_value
    )
    grid.done(att)
    own, core, first, second = grid.after(*cot_pieces)
    mine, theirs = pick(place, first, second)
    grid.done(mine)
    theirs = grid.swap_core(theirs)
    res, n2, n2t_keep, n2t_send = middle(place, x, *grid.after(att), w_out, gain_two)
    grid.done(n2)
    own, theirs = grid.after(own, theirs)
    branch, bt_keep, bt_send = branch_rows(place, (own, core, mine, theirs), items)
    hidden, gg, gu = hidden_rows(n2, branch, w_gate, w_up, w_down)

    pairs = width // LANES
    grads = []

    def attend():
        out = backward(
            len(grads) // 3, bias, cosine, sine, q, k, v, *grid.after(gatt), att, lse
        )
        grads.extend(out)
        grid.done(out[0])

    def weights(half, turn):
        chosen = grads[half * len(grads) // 2 :]
        kept, sent = attention_weights(place, half, chosen, *grid.after(normed), gwo, items)
        grid.done(kept)
        chunk = Reduction(grid, sent, turn, grid.bits - 1)
        chunk.keep(kept)
        return chunk

    def finish(*chunks):
        for chunk in chunks:
            chunk.finish()

    def start(*chunks):
        for chunk in chunks:
            if chunk.sent is not None:
                chunk.start()

    sent = grad_down(bt_send, hidden, items)
    grid.done(sent)
    down = Reduction(grid, sent, 0, grid.bits)
    start(down)
    down.keep(grad_down(*grid.after(bt_keep, hidden), items))
    sent = grad_columns(*grid.after(n2t_send, gg, gu), items)
    grid.done(sent)
    both = Reduction(grid, sent, 1, grid.bits)

    finish(down)
    start(down, both)
    both.keep(grad_columns(*grid.after(n2t_keep, gg, gu), items))
    gres, gatt, gwo, gsec = residual_grad(
        *grid.after(gg), gu, w_gate, w_up, res, branch, gain_two, w_out, att
    )
    grid.done(gres)

    finish(down, both)
    start(down, both)
    attend()
    attend()

    finish(down)
    start(down)
    attend()
    low = weights(0, 0)
    out_pieces = output_rows(place, *grid.after(hidden), w_down, res)
    grid.done(out_pieces[0])

    finish(down)
    start(low, down)
    own, core, side, across = out_pieces
    out_band = (own, grid.swap_core(core), side, grid.swap_core(across))
    attend()
    attend()

    finish(low)
    while not down.over:
        finish(down)
        start(down)
    finish(both)
    start(both, low)
    down_pieces = down.gather(down.held[0])
    attend()
    high = weights(1, 1)
    start(high)
    *in_pieces, gains = input_rows_grad(
        place, grads, w_query, w_key, w_value, *grid.after(x), gain, gres, gsec
    )
    grid.done(gains)
    high.gains, high.more = gains, grid.swap_core(gains)

    finish(high, low)
    start(low, high)
    own, core, side, across = in_pieces
    in_band = (own, grid.swap_core(core), side, grid.swap_core(across))
    finish(both)
    start(both)
    g_down = down_out(place, grid.after(*down_pieces))
    grid.done(g_down)

    def to_band(pieces):
        own, core, side, across = grid.after(*pieces)
        first, second = pair(place, side, across)
        grid.done(first)
        return own, core, grid.swap_x(first), grid.swap_x(second, only=0)

    finish(low, high)
    start(high, low)
    out_band = to_band(out_band)
    finish(both)
    start(both)
    in_band = to_band(in_band)
    finish(high)
    start(high)
    finish(low)
    start(low)
    while not low.over:
        finish(low)
        start(low)
    while high.stage < high.bits + 1:
        finish(high)
        start(high)
    values = grid.after(low.held, high.held, high.got, high.gains, high.more)
    kept, sent, gains = join_halves(place, *values, grid.bits - 1)
    grid.done(kept)
    got = grid.swap_item(sent, grid.bits - 1)
    more = grid.swap_item(gains, grid.bits - 1)
    while not both.over:
        finish(both)
        start(both)
    both_pieces = both.gather(both.held[0])
    output = band_rows(place, *grid.after(*out_band))
    grid.done(output)
    (block,) = combine(place, *grid.after(kept, got), 0, 0, False)
    grid.done(block)
    pieces = high.gather(block[0])
    grad_first, grad_second = gains_out(place, *grid.after(gains, more), items)
    grid.done(grad_first)
    g_gate, g_up = stacked_rows(place, grid.after(*both_pieces))
    grid.done(g_gate)
    input_grad = band_rows(place, *grid.after(*in_band))
    grid.done(input_grad)
    g_out, g_query, g_key, g_value = attention_out(place, grid.after(*pieces))
    return (
        output, input_grad, g_query, g_key, g_value, g_out, g_gate, g_up, g_down,
        grad_first[0], grad_second[0],
    )


def solution(mesh):
    rows = P("items", "band", None)
    in_specs = (rows, P("items")) + (P(),) * 9 + (rows,)
    out_specs = (rows, rows) + (P(None, "items"),) * 7 + (P("items"), P("items"))
    return jax.shard_map(
        functools.partial(body, Grid(mesh)),
        mesh=mesh, in_specs=in_specs, out_specs=out_specs, check_vma=False,
    )
```

```python
import functools
import math

import jax
import jax.numpy as jnp
from jax import lax
from jax.experimental import pallas as pl
from jax.experimental.pallas import tpu as pltpu
from jax.sharding import PartitionSpec as P

HEAD_DIM = 64
COLS = 24
EPSILON = 1e-05
LANES = 128
GROUP = 256
NEG = -1e30
AXES = ("items", "band")
BF16 = jnp.bfloat16
F32 = jnp.float32


def dot_nn(a, b):
    return lax.dot_general(a, b, (((1,), (0,)), ((), ())), preferred_element_type=F32)


def dot_nt(a, b):
    return lax.dot_general(a, b, (((1,), (1,)), ((), ())), preferred_element_type=F32)


def dot_tn(a, b):
    return lax.dot_general(a, b, (((0,), (0,)), ((), ())), preferred_element_type=F32)


def rope_tables(slots):
    half = HEAD_DIM // 2
    frequency = jnp.exp(
        -math.log(10000.0) * (2.0 * jnp.arange(half, dtype=F32) / HEAD_DIM)
    )
    angles = jnp.arange(slots, dtype=F32)[:, None] * frequency[None, :]
    cosine, sine = jnp.cos(angles), jnp.sin(angles)
    return (
        jnp.concatenate([cosine] * 4, axis=1),
        jnp.concatenate([-sine, sine, -sine, sine], axis=1),
    )


def turn(z, cosine, sine):
    lane = lax.broadcasted_iota(jnp.int32, z.shape, 1)
    low = (lane % HEAD_DIM) < HEAD_DIM // 2
    other = jnp.where(
        low, pltpu.roll(z, LANES - HEAD_DIM // 2, 1), pltpu.roll(z, HEAD_DIM // 2, 1)
    )
    return z * cosine + other * sine


def mask_bias(slots, tokens):
    row = lax.broadcasted_iota(jnp.int32, (slots, slots), 0)
    column = lax.broadcasted_iota(jnp.int32, (slots, slots), 1)
    return jnp.where((column <= row) & (column < tokens), 0.0, NEG).astype(F32)


def row_blocks(slots):
    cut = slots // 2 // LANES * LANES
    return ((0, cut, cut), (cut, slots - cut, slots)) if cut else ((0, slots, slots),)


BAND, CORE, SIDE, ITEM, HEIGHTS = range(5)


def tokens_of(place_ref):
    return place_ref[HEIGHTS + jnp.minimum(place_ref[BAND], 2)] * COLS


def join(place_ref, pieces, out_ref):
    band = place_ref[BAND]
    size = pieces[0].shape[0]
    for n, piece in enumerate(pieces):
        start = pl.multiple_of((band ^ n) * size, 16)
        out_ref[pl.ds(start, size), :] = piece[...]


def forward_kernel(
    place_ref, p0_ref, p1_ref, p2_ref, p3_ref, gain_ref, cos_ref, sin_ref, wq_ref, wk_ref, wv_ref,
    x_ref, q_ref, k_ref, v_ref, lse_ref, att_ref, normed_scr, bias_scr,
):
    slots, width = x_ref.shape
    join(place_ref, (p0_ref, p1_ref, p2_ref, p3_ref), x_ref)
    x = x_ref[...].astype(F32)
    r1 = lax.rsqrt(jnp.mean(x * x, axis=-1, keepdims=True) + EPSILON)
    normed_scr[...] = (x * r1 * gain_ref[...]).astype(BF16)
    bias_scr[...] = mask_bias(slots, tokens_of(place_ref))

    def group(g, carry):
        columns = pl.ds(pl.multiple_of(g * GROUP, GROUP), GROUP)
        normed = normed_scr[...]
        cosine, sine = cos_ref[...], sin_ref[...]
        q_all = dot_nn(normed, wq_ref[:, columns])
        k_all = dot_nn(normed, wk_ref[:, columns])
        v_ref[:, columns] = dot_nn(normed, wv_ref[:, columns]).astype(BF16)
        for p in range(GROUP // LANES):
            cut = slice(p * LANES, (p + 1) * LANES)
            place = pl.ds(pl.multiple_of(g * GROUP + p * LANES, LANES), LANES)
            q_ref[:, place] = (turn(q_all[:, cut], cosine, sine) * HEAD_DIM ** (-0.5)).astype(BF16)
            k_ref[:, place] = turn(k_all[:, cut], cosine, sine).astype(BF16)
        return carry

    lax.fori_loop(0, width // GROUP, group, 0)

    def pair(p, carry):
        place = pl.ds(pl.multiple_of(p * LANES, LANES), LANES)
        q2, k2, v2 = q_ref[:, place], k_ref[:, place], v_ref[:, place]
        low = lax.broadcasted_iota(jnp.int32, q2.shape, 1) < HEAD_DIM
        zero = jnp.zeros_like(q2)
        heads = jnp.where(low, q2, zero), jnp.where(low, zero, q2)
        v_ext = jnp.concatenate([v2, jnp.ones_like(v2)], axis=1)
        for start, size, keys in row_blocks(slots):
            rows = slice(start, start + size)
            bias = bias_scr[rows, :keys]
            s = dot_nt(jnp.concatenate([q[rows] for q in heads], axis=0), k2[:keys])
            s = s + jnp.concatenate([bias, bias], axis=0)
            m = jnp.max(s, axis=-1, keepdims=True)
            e = jnp.exp(s - m).astype(BF16)
            o = dot_nn(e, v_ext[:keys])
            total = o[:, LANES:]
            o = o[:, :LANES] / total
            log_total = m + jnp.log(total)
            att_ref[rows, place] = jnp.where(low[rows], o[:size], o[size:]).astype(BF16)
            lse_ref[rows, place] = jnp.where(low[rows], log_total[:size], log_total[size:])
        return carry

    lax.fori_loop(0, width // LANES, pair, 0)

def halves(place_ref, value_ref, units, keep_ref, send_ref):
    rows = value_ref.shape[0] // units // 2
    for n in range(units):
        for ref, core in ((keep_ref, place_ref[CORE]), (send_ref, 1 - place_ref[CORE])):
            start = pl.multiple_of((2 * n + core) * rows, 16)
            ref[n * rows : (n + 1) * rows, :] = value_ref[pl.ds(start, rows), :]


def middle_kernel(
    place_ref, x_ref, att_ref, wo_ref, gain_ref, res_ref, n2_ref, keep_ref, send_ref, scr
):
    res = x_ref[...].astype(F32) + dot_nn(att_ref[...], wo_ref[...])
    res_ref[...] = res
    r2 = lax.rsqrt(jnp.mean(res * res, axis=-1, keepdims=True) + EPSILON)
    n2 = res * r2 * gain_ref[...]
    n2_ref[...] = n2.astype(BF16)
    scr[...] = n2.T.astype(BF16)
    halves(place_ref, scr, 2, keep_ref, send_ref)


def middle(place, x, att, wo, gain):
    slots, width = x.shape
    rows = (slots, width)
    half = (width // 2, slots)
    return kernel_call(
        middle_kernel, "middle", (place, x, att, wo, gain),
        [(rows, F32), (rows, BF16), (half, BF16), (half, BF16)], [((width, slots), BF16)], scalars=1, limit=6,
    )


VMEM = pl.BlockSpec(memory_space=pltpu.VMEM)
SMEM = pl.BlockSpec(memory_space=pltpu.SMEM)
ANY = pl.BlockSpec(memory_space=pl.ANY)
HBM = pl.BlockSpec(memory_space=pltpu.HBM)


def kernel_call(
    body, name, operands, outs, scratch=(), limit=2, scalars=0, source=VMEM, target=VMEM,
    semaphores=0, weight=1,
):
    shapes = [jax.ShapeDtypeStruct(shape, kind) for shape, kind in outs]
    single = len(shapes) == 1
    scratch = [pltpu.VMEM(shape, kind) for shape, kind in scratch]
    if semaphores:
        scratch.append(pltpu.SemaphoreType.DMA((semaphores,)))
    return pl.pallas_call(
        body,
        in_specs=[SMEM] * scalars + [source] * (len(operands) - scalars),
        out_specs=target if single else [target] * len(shapes),
        out_shape=shapes[0] if single else shapes,
        scratch_shapes=scratch,
        compiler_params=pltpu.CompilerParams(vmem_limit_bytes=limit << 20),
        cost_estimate=pl.CostEstimate(flops=weight, bytes_accessed=1, transcendentals=0),
        name=name,
    )(*operands)


def forward(place, pieces, gain, cosine, sine, wq, wk, wv):
    width = wq.shape[0]
    slots = 4 * pieces[0].shape[0]
    rows = (slots, width)
    return kernel_call(
        forward_kernel, "attention_forward",
        (place, *pieces, gain, cosine, sine, wq, wk, wv),
        [(rows, BF16)] * 4 + [(rows, F32), (rows, BF16), (rows, BF16), ((slots, slots), F32)], scalars=1, limit=8,
    )


def branch_kernel(
    units, place_ref, p0_ref, p1_ref, p2_ref, p3_ref, branch_ref, keep_ref, send_ref, scr
):
    join(place_ref, (p0_ref, p1_ref, p2_ref, p3_ref), branch_ref)
    value = branch_ref[...].astype(F32)
    slot = lax.broadcasted_iota(jnp.int32, value.shape, 0)
    counted = jnp.where(place_ref[BAND] < 3, tokens_of(place_ref), 0)
    value = jnp.where(slot < counted, value, 0.0)
    branch_ref[...] = value.astype(BF16)
    scr[...] = value.T.astype(BF16)
    halves(place_ref, scr, units, keep_ref, send_ref)


def branch_rows(place, pieces, shards):
    band_slots, width = pieces[0].shape
    slots = 4 * band_slots
    half = (width // 2, slots)
    units = shards if (width // shards) % 32 == 0 else 1
    return kernel_call(
        functools.partial(branch_kernel, units), "branch_rows", (place, *pieces),
        [((slots, width), BF16), (half, BF16), (half, BF16)], [((width, slots), BF16)],
        scalars=1, limit=4,
    )


def hidden_kernel(n2_ref, branch_ref, wg_ref, wu_ref, wd_ref, hid_ref, gg_ref, gu_ref):
    def block(j, carry):
        columns = pl.ds(pl.multiple_of(j * GROUP, GROUP), GROUP)
        n2 = n2_ref[...]
        gate = dot_nn(n2, wg_ref[:, columns])
        up = dot_nn(n2, wu_ref[:, columns])
        grad_hidden = dot_nt(branch_ref[...], wd_ref[columns, :])
        sig = jax.nn.sigmoid(gate)
        silu = gate * sig
        hid_ref[:, columns] = (silu * up).astype(BF16)
        gg_ref[:, columns] = (grad_hidden * up * (sig * (1.0 + gate * (1.0 - sig)))).astype(BF16)
        gu_ref[:, columns] = (grad_hidden * silu).astype(BF16)
        return carry

    lax.fori_loop(0, wg_ref.shape[1] // GROUP, block, 0)


def hidden_rows(n2, branch, wg, wu, wd):
    slots, width = n2.shape
    ff = wg.shape[1]
    return kernel_call(
        hidden_kernel, "hidden_rows", (n2, branch, wg, wu, wd), [((slots, ff), BF16)] * 3, limit=3,
    )


def columns_kernel(lhs_ref, gate_ref, up_ref, out_ref):
    _, shards, rows, step = out_ref.shape
    rows //= 2

    def two(n, carry):
        place = pl.ds(pl.multiple_of(2 * n * step, 2 * step), 2 * step)
        for side, ref in enumerate((gate_ref, up_ref)):
            out = dot_nn(lhs_ref[...], ref[:, place]).astype(BF16)
            for j in range(2):
                part = out[:, j * step : (j + 1) * step].reshape(2, rows, step)
                out_ref[:, 2 * n + j, side * rows : (side + 1) * rows, :] = part
        return carry

    lax.fori_loop(0, shards // 2, two, 0)


def grad_columns(lhs, gate, up, shards):
    half, slots = lhs.shape
    ff = gate.shape[1]
    step = ff // shards
    if step % LANES:
        parts = [
            dot_nn(lhs, value).astype(BF16).reshape(2, half // 2, shards, step) for value in (gate, up)
        ]
        return jnp.swapaxes(jnp.concatenate(parts, axis=1), 1, 2)
    return kernel_call(
        columns_kernel, "grad_columns", (lhs, gate, up), [((2, shards, half, step), BF16)], limit=4,
    )


def down_kernel(lhs_ref, rhs_ref, out_ref):
    _, shards, rows, half = out_ref.shape
    step = 2 * GROUP
    for start in range(0, 2 * half, step):
        out = dot_nn(lhs_ref[...], rhs_ref[:, start : start + step]).astype(BF16)
        side, at = divmod(start, half)
        out_ref[side, :, :, at : at + step] = out.reshape(shards, rows, step)


def grad_down(lhs, hidden, shards):
    half, slots = lhs.shape
    ff = hidden.shape[1]
    rows = half // shards
    if rows % 16:
        out = dot_nn(lhs, hidden).astype(BF16).reshape(shards, rows, 2, ff // 2)
        return jnp.transpose(out, (2, 0, 1, 3))
    return kernel_call(
        down_kernel, "grad_down", (lhs, hidden), [((2, shards, rows, ff // 2), BF16)], limit=4,
    )


def combine_blocks(step, turn, place_ref, held_ref, got_ref, out_refs):
    count = out_refs[0].shape[0]
    if step is None:
        at, mine = 0, None
    elif isinstance(step, tuple):
        bit, at = step
        mine = (place_ref[ITEM] >> bit) & 1
    else:
        by_item = (place_ref[CORE] ^ turn ^ step) & 1
        top = (2 * count).bit_length() - 2
        at = top * (1 - by_item)
        mine = by_item * (place_ref[ITEM] & 1) + (1 - by_item) * place_ref[SIDE]

    def one(j, carry):
        for value, out_ref in zip((mine, 1 - mine) if mine is not None else (None,), out_refs):
            if value is None:
                block = j
            else:
                block = ((j >> at) << (at + 1)) + (value << at) + (j & ((1 << at) - 1))
            out_ref[j] = (held_ref[block].astype(F32) + got_ref[block].astype(F32)).astype(BF16)
        return carry

    lax.fori_loop(0, count, one, 0)


def combine_kernel(steps, turns, place_ref, *refs):
    ins, outs = refs[: 2 * len(steps)], refs[2 * len(steps) :]
    for step, turn in zip(steps, turns):
        count = 1 if step is None else 2
        combine_blocks(step, turn, place_ref, ins[0], ins[1], outs[:count])
        ins, outs = ins[2:], outs[count:]


def combine(place, values, steps, turns):
    outs = []
    for (held, _), step in zip(values, steps):
        blocks, r, c = held.shape
        outs += [((blocks, r, c), BF16)] if step is None else [((blocks // 2, r, c), BF16)] * 2
    out = kernel_call(
        functools.partial(combine_kernel, steps, turns), "combine",
        (place, *(value for both in values for value in both)), outs, scalars=1, limit=4,
    )
    return list(out) if isinstance(out, (list, tuple)) else [out]


def join_kernel(bit, place_ref, low_ref, held_ref, got_ref, keep_ref, send_ref):
    value = (held_ref[...].astype(F32) + got_ref[...].astype(F32)).astype(BF16)
    mine = (place_ref[ITEM] >> bit) & 1
    rows = low_ref.shape[1]
    keep_ref[:, rows:, :] = value[:, rows:]
    send_ref[:, rows:, :] = value[:, rows:]
    for top in range(2):
        @pl.when(mine == top)
        def _():
            (keep_ref if top else send_ref)[:, :rows, :] = value[:, :rows]
            (send_ref if top else keep_ref)[:, :rows, :] = low_ref[...]


def join_halves(place, low, held, got, bit):
    return kernel_call(
        functools.partial(join_kernel, bit), "join_halves", (place, low, held, got),
        [(held.shape, BF16)] * 2, scalars=1, limit=3,
    )


def pair_kernel(place_ref, a_ref, b_ref, *out_refs):
    for core in range(2):
        @pl.when(place_ref[CORE] == core)
        def _():
            out_refs[core][...] = a_ref[...]
            out_refs[1 - core][...] = b_ref[...]


def pair(place, a, b):
    return kernel_call(
        pair_kernel, "pair", (place, a, b), [(a.shape, a.dtype)] * 2, scalars=1, limit=1,
    )


def pick_kernel(place_ref, got_ref, mine_ref, theirs_ref):
    left = 1 - place_ref[SIDE]
    mine_ref[...] = got_ref[left * place_ref[CORE]]
    theirs_ref[...] = got_ref[left * (1 - place_ref[CORE])]


def pick(place, got):
    return kernel_call(
        pick_kernel, "pick", (place, got), [(got.shape[1:], got.dtype)] * 2, scalars=1, limit=1,
    )


def take_kernel(place_ref, rows_ref, own_ref, other_ref, far_ref):
    side, core = place_ref[SIDE], place_ref[CORE]
    far_ref[0] = rows_ref[jnp.where(side == 0, 2, 0)]
    far_ref[1] = rows_ref[jnp.where(side == 0, 2, 1)]
    other_ref[...] = rows_ref[jnp.where(side == 0, 1 - core, 2)]
    own_ref[...] = rows_ref[jnp.where(side == 0, core, 2)]


def take(place, rows):
    _, size, width = rows.shape
    kind = rows.dtype
    return kernel_call(
        take_kernel, "take", (place, rows),
        [((size, width), kind), ((size, width), kind), ((2, size, width), kind)], scalars=1, limit=1,
    )


def output_kernel(place_ref, hid_ref, wd_ref, res_ref, p0_ref, p1_ref, p2_ref, p3_ref, scr):
    out = res_ref[...] + dot_nn(hid_ref[...], wd_ref[...])
    slot = lax.broadcasted_iota(jnp.int32, out.shape, 0)
    scr[...] = jnp.where(slot < tokens_of(place_ref), out, 0.0).astype(BF16)
    part(place_ref, scr, (p0_ref, p1_ref, p2_ref, p3_ref))


def part(place_ref, value_ref, pieces):
    band = place_ref[BAND]
    size = pieces[0].shape[0]
    for n, piece in enumerate(pieces):
        start = pl.multiple_of((band ^ n) * size, 16)
        piece[...] = value_ref[pl.ds(start, size), :]


def output_rows(place, hidden, wd, res):
    slots, width = res.shape
    return kernel_call(
        output_kernel, "output_rows", (place, hidden, wd, res),
        [((slots // 4, width), BF16)] * 4, [((slots, width), BF16)], scalars=1, limit=5,
    )


def copy_all(pairs, sems):
    copies = [
        pltpu.make_async_copy(source, target, sems.at[n]) for n, (source, target) in enumerate(pairs)
    ]
    for copy in copies:
        copy.start()
    for copy in copies:
        copy.wait()


def band_kernel(place_ref, own_ref, core_ref, first_ref, second_ref, out_ref, sems):
    for core in range(2):
        own, other = (own_ref, core_ref) if core == 0 else (core_ref, own_ref)
        for side, rows in enumerate(((own, other, first_ref), (first_ref, second_ref, own))):
            @pl.when((place_ref[SIDE] == side) & (place_ref[CORE] == core))
            def _():
                copy_all([(row, out_ref.at[n]) for n, row in enumerate(rows)], sems)


def band_rows(place, own, core, first, second):
    size, width = own.shape
    return kernel_call(
        band_kernel, "band_rows", (place, own, core, first, second),
        [((3, size, width), BF16)], scalars=1, limit=1, target=ANY, semaphores=3,
    )


def rows_kernel(place_ref, p0_ref, p1_ref, p2_ref, p3_ref, gate_ref, up_ref, scr, sems):
    half = p0_ref.shape[0] // 2
    for n, piece in enumerate((p0_ref, p1_ref, p2_ref, p3_ref)):
        start = pl.multiple_of((place_ref[BAND] ^ n) * half, 8)
        scr[0, pl.ds(start, half), :] = piece[:half, :].astype(F32)
        scr[1, pl.ds(start, half), :] = piece[half:, :].astype(F32)
    copy_all([(scr.at[0], gate_ref), (scr.at[1], up_ref)], sems)


def stacked_rows(place, pieces):
    r, c = pieces[0].shape
    out = ((2 * r, c), F32)
    return kernel_call(
        rows_kernel, "weight_rows", (place, *pieces), [out, out], [((2, 2 * r, c), F32)], scalars=1, limit=4, target=ANY, semaphores=2,
    )


def down_out_kernel(place_ref, p0_ref, p1_ref, p2_ref, p3_ref, out_ref, scr, out_scr, sems):
    for n, piece in enumerate((p0_ref, p1_ref, p2_ref, p3_ref)):
        scr[place_ref[BAND] ^ n] = piece[...]
    r, c = p0_ref.shape
    for side in range(2):
        for core in range(2):
            out_scr[core * r : (core + 1) * r, side * c : (side + 1) * c] = (
                scr[2 * side + core].astype(F32)
            )
    copy_all([(out_scr, out_ref)], sems)


def down_out(place, pieces):
    r, c = pieces[0].shape
    shape = (2 * r, 2 * c)
    return kernel_call(
        down_out_kernel, "weight_down", (place, *pieces), [(shape, F32)],
        [((4, r, c), BF16), (shape, F32)], limit=4, scalars=1, target=ANY, semaphores=1,
    ).T


def attention_out_kernel(half, place_ref, p0_ref, p1_ref, p2_ref, p3_ref, *refs):
    outs, first_ref, second_ref, (scr, out_scr, sems) = refs[:4], refs[4], refs[5], refs[6:]
    for n, piece in enumerate((p0_ref, p1_ref, p2_ref, p3_ref)):
        scr[place_ref[BAND] ^ n] = piece[...]
    rows = out_scr.shape[1]
    out_scr[...] = scr[:, :rows, :].astype(F32)
    gains = scr[0, rows:, :].astype(F32)
    upper = place_ref[ITEM] >= half
    for n, ref in enumerate((first_ref, second_ref)):
        ref[...] = jnp.where(upper, gains[n : n + 1, :rows], gains[n + 2 : n + 3, :rows])
    copy_all([(out_scr.at[n], outs[n]) for n in range(4)], sems)


def attention_out(place, pieces, shards):
    r, c = pieces[0].shape
    share = c // shards
    outs = pl.pallas_call(
        functools.partial(attention_out_kernel, shards // 2),
        in_specs=[SMEM] + [VMEM] * 4,
        out_specs=[ANY] * 4 + [VMEM] * 2,
        out_shape=[jax.ShapeDtypeStruct((share, c), F32)] * 4
        + [jax.ShapeDtypeStruct((1, share), F32)] * 2,
        scratch_shapes=[
            pltpu.VMEM((4, r, c), BF16), pltpu.VMEM((4, share, c), F32), pltpu.SemaphoreType.DMA((4,)),
        ],
        compiler_params=pltpu.CompilerParams(vmem_limit_bytes=4 << 20),
        cost_estimate=pl.CostEstimate(flops=1, bytes_accessed=1, transcendentals=0),
        name="weight_attention",
    )(place, *pieces)
    return [out.T for out in outs[:4]], outs[4][0], outs[5][0]


def residual_kernel(
    gg_ref, gu_ref, wg_ref, wu_ref, res_ref, branch_ref, gain_ref, wo_ref, att_ref,
    gres_ref, gatt_ref, gwo_ref, gsec_ref, gn_scr, low_scr, turned_scr,
):
    slots, width = res_ref.shape

    def columns(n, carry):
        place = pl.ds(pl.multiple_of(n * GROUP, GROUP), GROUP)
        gn_scr[:, place] = dot_nt(gg_ref[...], wg_ref[place, :]) + dot_nt(gu_ref[...], wu_ref[place, :])
        return carry

    lax.fori_loop(0, width // GROUP, columns, 0)
    size = slots // 3

    def rows(n, total):
        place = pl.ds(pl.multiple_of(n * size, 16), size)
        gn, res = gn_scr[place, :], res_ref[place, :]
        r2 = lax.rsqrt(jnp.mean(res * res, axis=-1, keepdims=True) + EPSILON)
        weighted = gain_ref[...] * gn
        inner = jnp.mean(res * weighted, axis=-1, keepdims=True)
        gres = branch_ref[place, :].astype(F32) + r2 * weighted - res * (r2 * r2 * r2) * inner
        gres_ref[place, :] = gres
        low_scr[place, :] = gres.astype(BF16)
        return total + jnp.sum(gn * res * r2, axis=0, keepdims=True)

    gsec_ref[...] = lax.fori_loop(0, 3, rows, jnp.zeros((1, width), F32))
    turned_scr[...] = low_scr[...].T

    def products(n, carry):
        place = pl.ds(pl.multiple_of(n * GROUP, GROUP), GROUP)
        gatt_ref[:, place] = dot_nt(low_scr[...], wo_ref[place, :]).astype(BF16)
        gwo_ref[:, place] = dot_nn(turned_scr[...], att_ref[:, place]).astype(BF16)
        return carry

    lax.fori_loop(0, width // GROUP, products, 0)


def residual_grad(gg, gu, wg, wu, res, branch, gain, wo, att):
    slots, width = res.shape
    ff = gg.shape[1]
    rows = (slots, width)
    return kernel_call(
        residual_kernel, "residual_grad", (gg, gu, wg, wu, res, branch, gain, wo, att),
        [(rows, F32), (rows, BF16), ((width, width), BF16), ((1, width), F32)],
        [(rows, F32), (rows, BF16), ((width, slots), BF16)], limit=7,
    )


def backward_kernel(
    pair_ref, bias_ref, cos_ref, sin_ref, q_ref, k_ref, v_ref, gatt_ref, att_ref, lse_ref,
    dq_ref, dk_ref, dv_ref,
):
    slots = q_ref.shape[0]
    cosine, sine = cos_ref[...], -sin_ref[...]
    place = pl.ds(pl.multiple_of(pair_ref[0] * LANES, LANES), LANES)
    k2, v2 = k_ref[:, place], v_ref[:, place]
    low_k = lax.broadcasted_iota(jnp.int32, k2.shape, 1) < HEAD_DIM
    none = jnp.zeros_like(k2)
    k_of = (jnp.where(low_k, k2, none), jnp.where(low_k, none, k2))
    dk = jnp.zeros((slots, LANES), F32)
    dv = jnp.zeros((slots, LANES), F32)
    for start, size, keys in row_blocks(slots):
        rows = slice(start, start + size)
        q2, do2 = q_ref[rows, place], gatt_ref[rows, place]
        prod = do2.astype(F32) * att_ref[rows, place].astype(F32)
        lse2 = lse_ref[rows, place]
        low = low_k[rows]
        zero = jnp.zeros_like(q2)
        dq = jnp.zeros((size, LANES), F32)
        dk_part = jnp.zeros((keys, LANES), F32)
        dv_part = jnp.zeros((keys, LANES), F32)
        for head in range(2):
            mine = low if head == 0 else jnp.logical_not(low)
            qh = jnp.where(mine, q2, zero)
            doh = jnp.where(mine, do2, zero)
            delta = jnp.sum(jnp.where(mine, prod, 0.0), axis=-1, keepdims=True)
            lse = lse2[:, head * HEAD_DIM : head * HEAD_DIM + 1]
            s = dot_nt(qh, k2[:keys]) + bias_ref[rows, :keys]
            prob = jnp.exp(s - lse)
            dp = dot_nt(doh, v2[:keys])
            ds = (prob * (dp - delta)).astype(BF16)
            prob = prob.astype(BF16)
            dv_part += dot_tn(prob, doh)
            dk_part += dot_tn(ds, qh)
            dq += dot_nn(ds, k_of[head][:keys])
        dq_ref[rows, :] = (
            turn(dq, cosine[rows], sine[rows]) * HEAD_DIM ** (-0.5)
        ).astype(BF16)
        if keys < slots:
            pad = jnp.zeros((slots - keys, LANES), F32)
            dk_part = jnp.concatenate([dk_part, pad], axis=0)
            dv_part = jnp.concatenate([dv_part, pad], axis=0)
        dk += dk_part
        dv += dv_part
    dk_ref[...] = turn(dk, cosine, sine).astype(BF16)
    dv_ref[...] = dv.astype(BF16)


def backward(p, bias, cosine, sine, q, k, v, gatt, att, lse):
    slots, width = q.shape
    return kernel_call(
        backward_kernel, "attention_backward",
        (jnp.full((1,), p, jnp.int32), bias, cosine, sine, q, k, v, gatt, att, lse),
        [((slots, LANES), BF16)] * 3, scalars=1, limit=6,
    )


GAIN_ROWS = 8


def gain_rows(gains, shards, i):
    share = gains.shape[1] // shards
    mine = gains if i == 0 else pltpu.roll(gains, gains.shape[1] - i * share, 1)
    i += shards // 2
    other = pltpu.roll(gains, gains.shape[1] - i * share, 1)
    return jnp.concatenate([other[:2], mine[:2], jnp.zeros((4, gains.shape[1]), F32)], axis=0)


def attention_weights_kernel(shards, *refs):
    (place_ref, half_ref), refs = refs[:2], refs[2:]
    refs, (keep_ref, send_ref, grad_scr, out_scr) = refs[:-4], refs[-4:]
    grads, normed_ref, gwo_ref = refs[:9], refs[9], refs[10]
    _, count, share, width = keep_ref.shape
    share -= GAIN_ROWS if shards else 0
    rows = count * share
    for n in range(3):
        for p, ref in enumerate(grads[n::3]):
            grad_scr[n, :, p * LANES : (p + 1) * LANES] = ref[...]
    start = pl.multiple_of(half_ref[0] * rows, 16)
    out_scr[0, :, :share] = gwo_ref[pl.ds(start, rows), :].reshape(count, share, width)

    def weight(n, carry):
        value = dot_tn(grad_scr[n], normed_ref[...]).astype(BF16)
        out_scr[n + 1, :, :share] = value.reshape(count, share, width)
        return carry

    lax.fori_loop(0, 3, weight, 0)
    if shards:
        out_scr[1:, :, share:] = jnp.zeros((3, count, GAIN_ROWS, width), BF16)
        for i in range(count):
            out_scr[0, i, share:] = gain_rows(refs[11][...], shards, i).astype(BF16)

    def split(n, carry):
        side, i = n // count, n % count
        keep_ref[side, i] = out_scr[2 * side + place_ref[CORE], i]
        send_ref[side, i] = out_scr[2 * side + 1 - place_ref[CORE], i]
        return carry

    lax.fori_loop(0, 2 * count, split, 0)


def attention_weights(place, half, grads, normed, gwo, shards, gains=None):
    slots, width = normed.shape
    count, share = shards // 2, width // shards
    if share % 16:
        parts = [jnp.concatenate(grads[n::3], axis=1) for n in range(3)]
        weights = [dot_tn(value, normed).astype(BF16) for value in parts]
        rows = width // 2
        weights = jnp.stack([gwo[half * rows : (half + 1) * rows], *weights])
        parts = weights.reshape(2, 2, count, share, width)
        if gains is not None:
            table = gains[:2].reshape(2, 2, count, share)
            table = jnp.concatenate([table[:, 1], table[:, 0]])
            table = jnp.pad(jnp.swapaxes(table, 0, 1), ((0, 0), (0, 4), (0, width - share)))
            table = jnp.stack([table, *[jnp.zeros_like(table)] * 3]).reshape(2, 2, *table.shape)
            parts = jnp.concatenate([parts, table.astype(BF16)], axis=3)
        return [
            lax.dynamic_index_in_dim(parts, core, 1, keepdims=False)
            for core in (place[CORE], 1 - place[CORE])
        ]
    extra = () if gains is None else (gains,)
    shape = (2, count, share + (GAIN_ROWS if extra else 0), width)
    return kernel_call(
        functools.partial(attention_weights_kernel, shards if extra else 0), "attention_weights",
        (place, jnp.full((1,), half, jnp.int32), *grads, normed, gwo, *extra), [(shape, BF16)] * 2,
        [((3, slots, width // 2), BF16), ((4, *shape[1:]), BF16)], scalars=2, limit=9,
    )


def input_kernel(*refs):
    place_ref, refs = refs[0], refs[1:]
    count = len(refs) - 15
    grads, refs = refs[:count], refs[count:]
    wq_ref, wk_ref, wv_ref, x_ref, gain_ref, gres_ref, gsec_ref = refs[:7]
    pieces, (gains_ref, scr, gn_scr, grad_scr) = refs[7:11], refs[11:]
    slots, width = x_ref.shape
    for n in range(3):
        for p, ref in enumerate(grads[n::3]):
            grad_scr[n, :, p * LANES : (p + 1) * LANES] = ref[...]

    def columns(n, carry):
        place = pl.ds(pl.multiple_of(n * GROUP, GROUP), GROUP)
        gn_scr[:, place] = (
            dot_nt(grad_scr[0], wq_ref[place, :])
            + dot_nt(grad_scr[1], wk_ref[place, :])
            + dot_nt(grad_scr[2], wv_ref[place, :])
        )
        return carry

    lax.fori_loop(0, width // GROUP, columns, 0)
    size = slots // 3

    def rows(n, total):
        place = pl.ds(pl.multiple_of(n * size, 16), size)
        gn, x = gn_scr[place, :], x_ref[place, :].astype(F32)
        r1 = lax.rsqrt(jnp.mean(x * x, axis=-1, keepdims=True) + EPSILON)
        weighted = gain_ref[...] * gn
        inner = jnp.mean(x * weighted, axis=-1, keepdims=True)
        scr[place, :] = (
            gres_ref[place, :] + r1 * weighted - x * (r1 * r1 * r1) * inner
        ).astype(BF16)
        return total + jnp.sum(gn * x * r1, axis=0, keepdims=True)

    first = lax.fori_loop(0, 3, rows, jnp.zeros((1, width), F32))
    part(place_ref, scr, pieces)
    gains_ref[...] = jnp.concatenate([first, gsec_ref[...], jnp.zeros((6, width), F32)], axis=0)


def input_rows_grad(place, grads, wq, wk, wv, x, gain, gres, gsec):
    slots, width = x.shape
    return kernel_call(
        input_kernel, "input_grad", (place, *grads, wq, wk, wv, x, gain, gres, gsec),
        [((slots // 4, width), BF16)] * 4 + [((8, width), F32)],
        [((slots, width), BF16), ((slots, width), F32), ((3, slots, width), BF16)],
        scalars=1, limit=9,
    )


class Grid:
    def __init__(self, mesh):
        self.items = mesh.shape["items"]
        self.band = mesh.shape["band"]
        self.bits = self.items.bit_length() - 1

    def setup(self):
        self.i = lax.axis_index("items")
        self.b = lax.axis_index("band")
        self.core = self.b % 2
        self.x = self.b // 2
        self.y = self.i % 2
        self.last = ()

    def swap(self, value, partner):
        (value,) = self.after(value)
        pairs = []
        for i in range(self.items):
            for b in range(self.band):
                j, c = partner(i, b)
                pairs.append((i * self.band + b, j * self.band + c))
        return lax.ppermute(value, AXES, pairs)

    def swap_core(self, value):
        return self.swap(value, lambda i, b: (i, b ^ 1))

    def swap_x(self, value):
        return self.swap(value, lambda i, b: (i, b ^ 2))

    def swap_item(self, value, bit):
        return self.swap(value, lambda i, b: (i ^ (1 << bit), b))

    def swap_xy(self, value, turn):
        return self.swap(value, lambda i, b: (i ^ 1, b) if (b ^ turn) & 1 else (i, b ^ 2))

    def after(self, *values):
        if not self.last:
            return values
        tied = lax.optimization_barrier((values, self.last))
        return tied[0]

    def done(self, *values):
        self.last = values

    def also(self, *values):
        self.last = (*self.last, *values)


class Reduction:
    def __init__(self, grid, sent, turn, steps):
        self.grid, self.turn, self.steps = grid, turn, list(steps)
        flat = lambda value: value.reshape(-1, *value.shape[2:])
        self.sent = flat(sent)
        self.now = "core"

    @property
    def over(self):
        return self.now is None

    def keep(self, kept):
        self.held = kept.reshape(-1, *kept.shape[2:])
        self.grid.done(self.held)

    def exchange(self, value):
        grid = self.grid
        if self.now == "core":
            return grid.swap_core(value)
        if isinstance(self.now, tuple):
            return grid.swap_x(value) if self.now[0] == "x" else grid.swap_item(value, self.now[0])
        return grid.swap_xy(value, self.turn ^ self.now)

    def start(self):
        if self.sent is None:
            return
        self.got = self.exchange(self.sent)
        self.sent = None

    def gather(self, block):
        grid = self.grid
        return block, grid.swap_core(block), grid.swap_x(block)


def finish(*chunks):
    grid = chunks[0].grid
    values = grid.after(*((chunk.held, chunk.got) for chunk in chunks))
    for chunk in chunks:
        chunk.now = chunk.steps.pop(0) if chunk.steps else None
    out = combine(
        grid.place, values, [chunk.now for chunk in chunks], [chunk.turn for chunk in chunks]
    )
    for chunk in chunks:
        chunk.held = out.pop(0)
        chunk.sent = None if chunk.over else out.pop(0)
    grid.done(chunks[0].held)


def gather_last(grid, pieces):
    block, core, side = pieces
    return block, core, side, grid.swap_core(side)


def body(
    grid, activations, heights, w_query, w_key, w_value, w_out, w_gate, w_up, w_down,
    first_gain, second_gain, cotangent,
):
    grid.setup()
    items = grid.items
    _, band_slots, width = activations.shape
    slots = band_slots * grid.band
    ff = w_gate.shape[1]
    share = width // items
    place = jnp.stack([grid.b, grid.core, grid.x, grid.i]).astype(jnp.int32)
    place = jnp.concatenate([place, heights])
    grid.place = place
    own, other, far = take(place, activations)
    got = grid.swap_x(far)
    core = grid.swap_core(other)
    (cotangent,) = lax.optimization_barrier((cotangent, far))[:1]
    cot_own, cot_other, far = take(place, cotangent)
    cot_got = grid.swap_x(far)
    cosine, sine = rope_tables(slots)
    gain, gain_two = first_gain[None, :], second_gain[None, :]

    got, cosine, sine, gain, gain_two, _ = lax.optimization_barrier(
        (got, cosine, sine, gain, gain_two, far)
    )
    mine, theirs = pick(place, got)
    theirs = grid.swap_core(theirs)
    grid.done(mine)
    x, q, k, v, lse, att, normed, bias = forward(
        place, (own, core, mine, theirs), gain, cosine, sine, w_query, w_key, w_value
    )
    grid.done(att)
    mine, theirs = pick(place, *grid.after(cot_got))
    grid.done(mine)
    own, core, theirs = cot_own, grid.swap_core(cot_other), grid.swap_core(theirs)
    res, n2, n2t_keep, n2t_send = middle(place, x, *grid.after(att), w_out, gain_two)
    grid.done(n2)
    core, theirs = grid.after(core, theirs)
    branch, bt_keep, bt_send = branch_rows(place, (own, core, mine, theirs), items)
    hidden, gg, gu = hidden_rows(n2, branch, w_gate, w_up, w_down)

    lines = [(bit, 0) for bit in range(1, grid.bits)]
    grads = []

    def attend():
        out = backward(
            len(grads) // 3, bias, cosine, sine, q, k, v, *grid.after(gatt), att, lse
        )
        grads.extend(out)
        grid.done(out[0])

    def weights(half, turn, gains=None):
        chosen = grads[half * len(grads) // 2 :]
        kept, sent = attention_weights(
            place, half, chosen, *grid.after(normed), gwo, items, gains
        )
        grid.done(kept)
        chunk = Reduction(grid, sent, turn, [0, 1, *lines[:-1]])
        chunk.keep(kept)
        return chunk

    def start(*chunks):
        for chunk in chunks:
            if chunk.sent is not None:
                chunk.start()

    def to_band(pieces):
        own, core, side, across = grid.after(*pieces)
        both = pair(place, side, across)
        grid.done(both[0])
        return own, core, both

    def across_cores(pieces):
        own, core, side, across = pieces
        return own, grid.swap_core(core), side, grid.swap_core(across)

    sent = grad_columns(n2t_send, gg, gu, items)
    grid.done(sent)
    both = Reduction(grid, sent, 1, [0, 1, *lines])
    start(both)
    sent = grad_down(*grid.after(bt_send, hidden), items)
    grid.done(sent)
    down = Reduction(grid, sent, 0, [*((bit, 1) for bit, _ in lines[:1]), 0, 1, *lines[1:]])
    start(down)
    both.keep(grad_columns(*grid.after(n2t_keep, gg, gu), items))
    down.keep(grad_down(*grid.after(bt_keep, hidden), items))

    finish(down, both)
    start(both, down)
    out_pieces = output_rows(place, *grid.after(hidden), w_down, res)
    grid.done(out_pieces[0])
    out_band = across_cores(out_pieces)
    gres, gatt, gwo, gsec = residual_grad(
        *grid.after(gg), gu, w_gate, w_up, res, branch, gain_two, w_out, att
    )
    grid.done(gres)
    out_own, out_core, far = to_band(out_band)
    out_first = grid.swap_x(far[0])
    attend()
    attend()
    attend()
    low = weights(0, 1)
    grid.also(out_first)

    finish(down, both)
    start(both, low)
    out_second = grid.swap_x(far[1])
    attend()
    attend()
    attend()
    *in_pieces, gains = input_rows_grad(
        place, grads, w_query, w_key, w_value, *grid.after(x), gain, gres, gsec
    )
    grid.done(gains)
    high = weights(1, 1, gains)

    grid.also(out_second)
    finish(both, low)
    start(low, both, down, high)
    in_band = across_cores(in_pieces)
    output = band_rows(place, *grid.after(out_own, out_core, out_first, out_second))
    grid.done(output)

    finish(down, both, low, high)
    start(high, low, both, down)
    in_own, in_core, in_far = to_band(in_band)

    while len(down.steps) > 1:
        finish(down)
        start(down)
    while len(both.steps) > 1:
        finish(both)
        start(both)
    finish(down, both, low, high)
    start(high, low, down)
    while not both.over:
        finish(both)
        start(both)
    while low.steps:
        finish(low)
        start(low)
    while down.steps:
        finish(down)
        start(down)
    finish(down, low, high)
    start(high)
    both_pieces = both.gather(both.held[0])
    down_pieces = down.gather(down.held[0])
    while high.steps:
        finish(high)
        start(high)
    down_pieces = gather_last(grid, grid.after(*down_pieces))
    both_pieces = gather_last(grid, grid.after(*both_pieces))
    grid.also(down_pieces[2], both_pieces[2])
    kept, sent = join_halves(
        place, *grid.after(low.held, high.held, high.got), grid.bits - 1
    )
    grid.done(kept)
    got = grid.swap_item(sent, grid.bits - 1)
    in_got = [grid.swap_x(piece) for piece in in_far]
    g_down = down_out(place, grid.after(*down_pieces))
    grid.done(g_down)
    g_gate, g_up = stacked_rows(place, grid.after(*both_pieces))
    grid.done(g_gate)
    (block,) = combine(place, [grid.after(kept, got)], [None], [0])
    grid.done(block)
    pieces = high.gather(block[0])
    input_grad = band_rows(place, *grid.after(in_own, in_core, *in_got))
    grid.done(input_grad)
    pieces = gather_last(grid, grid.after(*pieces))
    grads, grad_first, grad_second = attention_out(place, pieces, items)
    g_out, g_query, g_key, g_value = grads
    return (
        output, input_grad, g_query, g_key, g_value, g_out, g_gate, g_up, g_down,
        grad_first, grad_second,
    )


def solution(mesh):
    rows = P("items", "band", None)
    in_specs = (rows, P("items")) + (P(),) * 9 + (rows,)
    out_specs = (rows, rows) + (P(None, "items"),) * 7 + (P("items"), P("items"))
    return jax.shard_map(
        functools.partial(body, Grid(mesh)),
        mesh=mesh, in_specs=in_specs, out_specs=out_specs, check_vma=False,
    )
```
